32 devices in a mesh: vel: 2 (over core), sx: 4 (over y, x), sy: 4 (over z).
Axes of the slice: x: 2, y: 2, z: 4, core: 2. Of those that a mesh axis runs over, the one named last changes fastest.
Arguments:
- particle_distributions: bfloat16 [512, 32, 512], P('vel', 'sx', 'sy'), may hold values from 0.099609375 to 2
- integer_grid_displacements: int32 [2, 512], P(None, 'vel'), may hold values from -4 to 3, as said below
- leftover_shift_part: float32 [2, 512], P(None, 'vel'), may hold values from 0 to 1
- relaxing_frequency_dt: float32 [32, 512], P('sx', 'sy'), may hold values from 0.1 to 3
- solid_indicator: int32 [32, 512], P('sx', 'sy'), may hold values 0 or 1
- solid_heat_level: float32 [1], replicated, may hold values from 0.5 to 4
Outputs:
- advanced: bfloat16 [512, 32, 512], P('vel', 'sx', 'sy')
The draws below stay inside these ranges and needn't reach their ends.
Inputs may be any that keep to these rules, and one draw needn't show every extreme that they name: `integer_grid_displacements`: row 0 grows with the velocity's index by steps of at most one, up to a random step of one; row 1 is arbitrary. Both rows reach both ends.
All inputs are finite; a program needn't handle non-finite values. No bound on the sum of `solid_indicator` on one device may be relied on, other than what follows from the above.
Results may differ from the reference program's by a relative error of at most 0.0028.
Values may be sent and summed in bfloat16 or wider, within the bound.
A program may use at most 128 MiB of HBM per device.

```python
import math
import jax
import jax.numpy as jnp
from jax import lax

VD = 256
MAXS = 4
STEPS = 2
NV = 512
NX = 32
NY = 512


def draw_integer_grid_displacements(key, part):
    first_key = jax.random.fold_in(key, 11)
    second_key = jax.random.fold_in(key, 23)
    index = jnp.arange(NV, dtype=jnp.int32)
    along_x = index * (2 * MAXS) // NV - MAXS + jax.random.randint(first_key, (NV,), 0, 2, dtype=jnp.int32)
    along_x = jnp.minimum(along_x, MAXS - 1).at[0].set(-MAXS)
    along_y = jax.random.randint(second_key, (NV,), -MAXS, MAXS, dtype=jnp.int32)
    along_y = along_y.at[0].set(-MAXS).at[1].set(MAXS - 1)
    return jnp.stack([along_x, along_y]).astype(jnp.int32)


def set_ends(entries, own_key, least, top_value):
    spot = [jax.random.randint(jax.random.fold_in(own_key, axis), (), 0, length) for axis, length in enumerate(entries.shape)]
    main_axis = entries.shape.index(max(entries.shape))
    neighbour = spot[:main_axis] + [(spot[main_axis] + 1) % entries.shape[main_axis]] + spot[main_axis + 1:]
    return entries.at[tuple(spot)].set(least).at[tuple(neighbour)].set(top_value)


def levels(key, extent, cuts, smallest, high):
    gain = 1.0
    for position, parts in cuts:
        draws = jax.random.uniform(jax.random.fold_in(jax.random.fold_in(key, 6), position), (parts,), jnp.float32, smallest / len(cuts), high / len(cuts))
        gain = gain * jnp.repeat(jnp.exp(draws), extent[position] // parts).reshape((-1,) + (1,) * (len(extent) - 1 - position))
    return gain


def setup_inputs(seed: int = 0) -> dict:
    streams_of = jax.random.split(jax.random.key(seed), 7)
    particle_distributions = jnp.clip(jnp.exp(math.log(2.0) - 2.9996462 * jax.random.uniform(streams_of[0], (NV, NX, NY), jnp.float32) ** levels(streams_of[0], (NV, NX, NY), ((0, 2), (1, 4), (2, 4)), -0.2, 0.2)), 0.099609375, 2.0).astype(jnp.bfloat16)
    integer_grid_displacements = draw_integer_grid_displacements(jax.random.fold_in(streams_of[6], 71), 0)
    leftover_shift_part = jnp.clip(1.0 * jax.random.uniform(streams_of[2], (2, NV), jnp.float32) ** levels(streams_of[2], (2, NV), ((1, 2),), -0.2, 0.2), 0.0, 1.0)
    relaxing_frequency_dt = jnp.clip(jnp.exp(math.log(3.0) - 3.4011974 * jax.random.uniform(streams_of[3], (NX, NY), jnp.float32) ** levels(streams_of[3], (NX, NY), ((0, 4), (1, 4)), -0.2, 0.2)), 0.1, 3.0)
    solid_indicator = set_ends((jax.random.randint(streams_of[4], (NX, NY), 0, 6) < 1).astype(jnp.int32), jax.random.fold_in(streams_of[4], 1), 0, 1)
    solid_heat_level = jnp.clip(jnp.exp(jax.random.uniform(streams_of[5], (1,), jnp.float32, math.log(0.5), math.log(4.0))), 0.5, 4.0)
    return dict(particle_distributions=particle_distributions, integer_grid_displacements=integer_grid_displacements, leftover_shift_part=leftover_shift_part, relaxing_frequency_dt=relaxing_frequency_dt, solid_indicator=solid_indicator, solid_heat_level=solid_heat_level)


def shift_planes(planes, shifts, fracs, axis):
    def single(plane, moves, part):
        return (1.0 - part) * jnp.roll(plane, moves, axis) + part * jnp.roll(plane, moves + 1, axis)
    return jax.vmap(single)(planes, shifts, fracs)


def advect(planes, shifts, fracs):
    moved = shift_planes(planes.astype(jnp.float32), shifts[0], fracs[0], 0)
    return shift_planes(moved, shifts[1], fracs[1], 1)


def reference(particle_distributions, integer_grid_displacements, leftover_shift_part, relaxing_frequency_dt, solid_indicator, solid_heat_level):
    blocks = NV // VD
    speed = integer_grid_displacements.astype(jnp.float32) + leftover_shift_part
    square_accumulated = speed[0] * speed[0] + speed[1] * speed[1]
    wall_layout = jnp.exp(-square_accumulated / (2.0 * solid_heat_level[0]))
    wall_sum = jnp.sum(wall_layout)
    relax_rate = 1.0 - jnp.exp(-relaxing_frequency_dt)
    solid = solid_indicator > 0
    shift_b = integer_grid_displacements.reshape(2, blocks, VD).transpose(1, 0, 2)
    frac_b = leftover_shift_part.reshape(2, blocks, VD).transpose(1, 0, 2)
    speed_b = speed.reshape(2, blocks, VD).transpose(1, 0, 2)
    wall_b = wall_layout.reshape(blocks, VD)
    state = particle_distributions.reshape(blocks, VD, NX, NY)
    zeros = jnp.zeros((NX, NY), jnp.float32)
    for step in range(STEPS):
        def gather_moments(carry, item):
            planes, shifts, fracs, speeds = item
            moved = advect(planes, shifts, fracs)
            speed_x = speeds[0][:, None, None]
            speed_y = speeds[1][:, None, None]
            square_piece = speed_x * speed_x + speed_y * speed_y
            return (carry[0] + jnp.sum(moved, 0), carry[1] + jnp.sum(moved * speed_x, 0),
                    carry[2] + jnp.sum(moved * speed_y, 0), carry[3] + jnp.sum(moved * square_piece, 0)), None

        (density, flux_x, flux_y, energy), unused = lax.scan(
            gather_moments, (zeros, zeros, zeros, zeros), (state, shift_b, frac_b, speed_b))
        drift_x = flux_x / density
        drift_y = flux_y / density
        thermal = 0.5 * (energy / density - drift_x * drift_x - drift_y * drift_y)

        def profile_of(speeds):
            off_x = speeds[0][:, None, None] - drift_x
            off_y = speeds[1][:, None, None] - drift_y
            return jnp.exp(-(off_x * off_x + off_y * off_y) / (2.0 * thermal))

        def add_profile(carry, speeds):
            return carry + jnp.sum(profile_of(speeds), 0), None

        partition_sum, unused = lax.scan(add_profile, zeros, speed_b)

        def relax_block(item):
            planes, shifts, fracs, speeds, wall_part = item
            moved = advect(planes, shifts, fracs)
            profile = profile_of(speeds)
            relaxed = moved + relax_rate * (density * profile / partition_sum - moved)
            at_wall = density * wall_part[:, None, None] / wall_sum
            return jnp.where(solid, at_wall, relaxed).astype(jnp.bfloat16)

        state = lax.map(relax_block, (state, shift_b, frac_b, speed_b, wall_b))
    return state.reshape(NV, NX, NY)
```

```python
import functools
import math

import jax
import jax.numpy as jnp
from jax import lax
from jax.experimental import pallas as pl
from jax.experimental.pallas import tpu as pltpu
from jax.sharding import PartitionSpec as P

MAXS = 4
STEPS = 2
ROWS = 8
LANES = 128
GROUP = 16
SPAN = 24
LOG2E = math.log2(math.e)
F32 = jnp.float32
BF16 = jnp.bfloat16


def kernel(
    sizes,
    disp,
    frac,
    heat,
    x_ref,
    freq_ref,
    solid_ref,
    o_ref,
    ext,
    pext,
    pack_f,
    moved_ref,
    prof_ref,
    wall_ref,
    xsend,
    psend,
    csend,
    xrecv,
    precv,
    crecv,
    msend,
    mrecv,
    zsend,
    zrecv,
    xs_sem,
    xr_sem,
    ps_sem,
    pr_sem,
    cs_sem,
    cr_sem,
    ms_sem,
    mr_sem,
    zs_sem,
    zr_sem,
):
    nvel, nsx, nsy = sizes
    nv = disp.shape[1]
    groups = nv // GROUP
    vel = lax.axis_index("vel")
    sx = lax.axis_index("sx")
    sy = lax.axis_index("sy")
    up, down = lax.rem(sx + 1, nsx), lax.rem(sx + nsx - 1, nsx)
    right, left = lax.rem(sy + 1, nsy), lax.rem(sy + nsy - 1, nsy)
    peers = [lax.rem(vel + p, nvel) for p in range(1, nvel)]
    sources = [lax.rem(vel + nvel - p, nvel) for p in range(1, nvel)]

    def at(v, i, j):
        return (v, i, j)

    spatial = [
        at(vel, up, sy), at(vel, down, sy), at(vel, sx, right), at(vel, sx, left),
        at(vel, up, right), at(vel, up, left), at(vel, down, right), at(vel, down, left),
    ]
    barrier = pltpu.get_barrier_semaphore()
    for target in spatial + [at(p, sx, sy) for p in peers]:
        pl.semaphore_signal(barrier, inc=1, device_id=target, device_id_type=pl.DeviceIdType.MESH)

    lane = lax.broadcasted_iota(jnp.int32, (ROWS, LANES), 1)
    centered = jnp.where(lane < LANES // 2, lane, lane - LANES)
    slot = lane // 8
    from_left = lax.rem(lane, 8) < 4

    def remote(src, dst, send_sem, recv_sem, target):
        return pltpu.make_async_remote_copy(
            src_ref=src, dst_ref=dst, send_sem=send_sem, recv_sem=recv_sem,
            device_id=target, device_id_type=pl.DeviceIdType.MESH,
        )

    def halo_copies(step):
        copies = [
            remote(xsend.at[step, 0], xrecv.at[step, 0], xs_sem.at[step, 0], xr_sem.at[step, 0], spatial[0]),
            remote(xsend.at[step, 1], xrecv.at[step, 1], xs_sem.at[step, 1], xr_sem.at[step, 1], spatial[1]),
            remote(psend.at[step], precv.at[step, 0], ps_sem.at[step, 0], pr_sem.at[step, 0], spatial[2]),
            remote(psend.at[step], precv.at[step, 1], ps_sem.at[step, 1], pr_sem.at[step, 1], spatial[3]),
        ]
        for c in range(4):
            copies.append(
                remote(csend.at[step, c // 2], crecv.at[step, c], cs_sem.at[step, c], cr_sem.at[step, c], spatial[4 + c])
            )
        return copies

    def stow(step, g, planes):
        packed = None
        for k, plane in enumerate(planes):
            ext[pl.ds(pl.multiple_of((g * GROUP + k) * SPAN, 8) + 8, ROWS), :] = plane
            turned = pltpu.roll(plane, (8 * k + 4) % LANES, 1)
            packed = turned if packed is None else jnp.where(slot == k, turned, packed)
        pack_f[pl.ds(pl.multiple_of(g * ROWS, 8), ROWS), :] = packed
        for q in range(GROUP // 4):
            four = planes[4 * q: 4 * q + 4]
            base = pl.multiple_of(g * (GROUP * 4) + q * 16, 16)
            xsend[step, 0, pl.ds(base, 16), :] = jnp.concatenate([f[4:8] for f in four], 0).astype(BF16)
            xsend[step, 1, pl.ds(base, 16), :] = jnp.concatenate([f[0:4] for f in four], 0).astype(BF16)

    def finish_pack(step):
        psend[step] = pack_f[...].astype(BF16)
        for j in range(groups // 4):
            for side, first in ((0, 4), (1, 0)):
                pieces = [pack_f[(4 * j + i) * ROWS + first: (4 * j + i) * ROWS + first + 4, :] for i in range(4)]
                csend[step, side, 16 * j: 16 * j + 16, :] = jnp.concatenate(pieces, 0).astype(BF16)

    def unpack(step):
        def rows(q, carry):
            base = pl.multiple_of(q * 16, 16)
            low = xrecv[step, 0, pl.ds(base, 16), :].astype(F32)
            high = xrecv[step, 1, pl.ds(base, 16), :].astype(F32)
            for i in range(4):
                spot = pl.multiple_of((q * 4 + i) * SPAN, 8)
                ext[pl.ds(spot + 4, 4), :] = low[4 * i: 4 * i + 4]
                ext[pl.ds(spot + 16, 4), :] = high[4 * i: 4 * i + 4]
            return carry

        lax.fori_loop(0, nv // 4, rows, 0)
        for j in range(groups // 2):
            a = precv[step, 0, 16 * j: 16 * j + 16, :].astype(F32)
            b = precv[step, 1, 16 * j: 16 * j + 16, :].astype(F32)
            for i in range(2):
                spot = (2 * j + i) * SPAN
                pext[spot + 8: spot + 16, :] = jnp.where(from_left, a[8 * i: 8 * i + 8], b[8 * i: 8 * i + 8])
        pick = from_left[0:4]
        for j in range(groups // 4):
            parts = [crecv[step, c, 16 * j: 16 * j + 16, :].astype(F32) for c in range(4)]
            for i in range(4):
                spot = (4 * j + i) * SPAN
                cut = slice(4 * i, 4 * i + 4)
                pext[spot + 4: spot + 8, :] = jnp.where(pick, parts[0][cut], parts[1][cut])
                pext[spot + 16: spot + 20, :] = jnp.where(pick, parts[2][cut], parts[3][cut])

    def speeds(v):
        return disp[0, v].astype(F32) + frac[0, v], disp[1, v].astype(F32) + frac[1, v]

    def source(main, side, shift):
        low, high = jnp.minimum(-shift, 0), jnp.maximum(-shift, 0)
        return jnp.where((centered >= low) & (centered < high), side, main)

    def turn(plane, shift):
        return pltpu.roll(plane, jnp.where(shift < 0, shift + LANES, shift), 1)

    def transport(g, k):
        v = g * GROUP + k
        mx, my = disp[0, v], disp[1, v]
        a, b = frac[0, v], frac[1, v]
        start = v * SPAN + 8 - mx
        main = (1.0 - a) * ext[pl.ds(start, ROWS), :] + a * ext[pl.ds(start - 1, ROWS), :]
        pstart = g * SPAN + 8 - mx
        side = (1.0 - a) * pext[pl.ds(pstart, ROWS), :] + a * pext[pl.ds(pstart - 1, ROWS), :]
        side = pltpu.roll(side, (2 * LANES - 8 * k - 4) % LANES, 1)
        near = turn(source(main, side, my), my)
        far = turn(source(main, side, my + 1), my + 1)
        return (1.0 - b) * near + b * far

    def add_over_vel(step, count, sref, rref, ssem, rsem, values):
        for i, value in enumerate(values):
            sref[step, i * ROWS: (i + 1) * ROWS, :] = value
        copies = [
            remote(sref.at[step], rref.at[step, p], ssem.at[step, p], rsem.at[step, p], at(peers[p], sx, sy))
            for p in range(nvel - 1)
        ]
        for copy in copies:
            copy.start()
        for copy in copies:
            copy.wait()
        totals = []
        for i, value in enumerate(values):
            for p in range(nvel - 1):
                value = value + rref[step, p, i * ROWS: (i + 1) * ROWS, :]
            totals.append(value)
        return totals

    zero = jnp.zeros((ROWS, LANES), F32)
    relax = 1.0 - jnp.exp(-freq_ref[...])
    solid = solid_ref[...] > 0
    wall_scale = -LOG2E / (2.0 * (zero + heat[0]))

    def load_group(g, carry):
        planes = []
        for k in range(0, GROUP, 2):
            pair = x_ref[pl.ds(pl.multiple_of(g * (GROUP * ROWS) + k * ROWS, 16), 16), :].astype(F32)
            planes += [pair[0:8], pair[8:16]]
        stow(0, g, planes)
        return carry

    lax.fori_loop(0, groups, load_group, 0)
    finish_pack(0)
    pl.semaphore_wait(barrier, len(spatial) + nvel - 1)

    wall_sum = None
    for step in range(STEPS):
        copies = halo_copies(step)
        for copy in copies:
            copy.start()
        if step == 0:
            def wall_group(g, total):
                for k in range(GROUP):
                    v = g * GROUP + k
                    cx, cy = speeds(v)
                    w = jnp.exp2((cx * cx + cy * cy) * wall_scale)
                    wall_ref[pl.ds(pl.multiple_of(v * ROWS, 8), ROWS), :] = w
                    total = total + w
                return total

            wall_sum = lax.fori_loop(0, groups, wall_group, zero)
        for copy in copies:
            copy.wait()
        unpack(step)

        def moment_group(g, carry):
            density, flux_x, flux_y, energy = carry
            for k in range(GROUP):
                v = g * GROUP + k
                cx, cy = speeds(v)
                moved = transport(g, k)
                moved_ref[pl.ds(pl.multiple_of(v * ROWS, 8), ROWS), :] = moved
                density = density + moved
                flux_x = flux_x + moved * cx
                flux_y = flux_y + moved * cy
                energy = energy + moved * (cx * cx + cy * cy)
            return density, flux_x, flux_y, energy

        moments = list(lax.fori_loop(0, groups, moment_group, (zero, zero, zero, zero)))
        extra = [wall_sum] if step == 0 else [zero]
        totals = add_over_vel(step, 5, msend, mrecv, ms_sem, mr_sem, moments + extra)
        density, flux_x, flux_y, energy = totals[:4]
        if step == 0:
            wall_sum = totals[4]
        drift_x = flux_x / density
        drift_y = flux_y / density
        thermal = 0.5 * (energy / density - drift_x * drift_x - drift_y * drift_y)
        scale = -LOG2E / (2.0 * thermal)

        def profile_group(g, total):
            for k in range(GROUP):
                v = g * GROUP + k
                cx, cy = speeds(v)
                off_x = cx - drift_x
                off_y = cy - drift_y
                value = jnp.exp2((off_x * off_x + off_y * off_y) * scale)
                prof_ref[pl.ds(pl.multiple_of(v * ROWS, 8), ROWS), :] = value
                total = total + value
            return total

        partition = lax.fori_loop(0, groups, profile_group, zero)
        (partition,) = add_over_vel(step, 1, zsend, zrecv, zs_sem, zr_sem, [partition])
        keep = 1.0 - relax
        gain = relax * density / partition
        wall_gain = density / wall_sum

        def relax_group(g, carry):
            planes = []
            for k in range(GROUP):
                rows = pl.ds(pl.multiple_of((g * GROUP + k) * ROWS, 8), ROWS)
                gas = keep * moved_ref[rows, :] + gain * prof_ref[rows, :]
                planes.append(jnp.where(solid, wall_gain * wall_ref[rows, :], gas))
            for k in range(0, GROUP, 2):
                pair = jnp.concatenate(planes[k: k + 2], 0).astype(BF16)
                if step == STEPS - 1:
                    o_ref[pl.ds(pl.multiple_of((g * GROUP + k) * ROWS, 16), 16), :] = pair
                else:
                    pair = pair.astype(F32)
                    planes[k: k + 2] = [pair[0:8], pair[8:16]]
            if step < STEPS - 1:
                stow(step + 1, g, planes)
            return carry

        lax.fori_loop(0, groups, relax_group, 0)
        if step < STEPS - 1:
            finish_pack(step + 1)


def per_device(sizes, particle_distributions, disp, frac, freq, solid, heat):
    nv, rows, lanes = particle_distributions.shape
    assert rows == ROWS and lanes == LANES and nv % (4 * GROUP) == 0
    nvel = sizes[0]
    others = max(nvel - 1, 1)
    groups = nv // GROUP
    dma = pltpu.SemaphoreType.DMA
    vmem = pl.BlockSpec(memory_space=pltpu.VMEM)
    smem = pl.BlockSpec(memory_space=pltpu.SMEM)
    out = pl.pallas_call(
        functools.partial(kernel, sizes),
        out_shape=jax.ShapeDtypeStruct((nv * ROWS, LANES), BF16),
        in_specs=[smem, smem, smem, vmem, vmem, vmem],
        out_specs=vmem,
        scratch_shapes=[
            pltpu.VMEM((nv * SPAN, LANES), F32),
            pltpu.VMEM((groups * SPAN, LANES), F32),
            pltpu.VMEM((groups * ROWS, LANES), F32),
            pltpu.VMEM((nv * ROWS, LANES), F32),
            pltpu.VMEM((nv * ROWS, LANES), F32),
            pltpu.VMEM((nv * ROWS, LANES), F32),
            pltpu.VMEM((STEPS, 2, nv * MAXS, LANES), BF16),
            pltpu.VMEM((STEPS, groups * ROWS, LANES), BF16),
            pltpu.VMEM((STEPS, 2, groups * MAXS, LANES), BF16),
            pltpu.VMEM((STEPS, 2, nv * MAXS, LANES), BF16),
            pltpu.VMEM((STEPS, 2, groups * ROWS, LANES), BF16),
            pltpu.VMEM((STEPS, 4, groups * MAXS, LANES), BF16),
            pltpu.VMEM((STEPS, 5 * ROWS, LANES), F32),
            pltpu.VMEM((STEPS, others, 5 * ROWS, LANES), F32),
            pltpu.VMEM((STEPS, ROWS, LANES), F32),
            pltpu.VMEM((STEPS, others, ROWS, LANES), F32),
            dma((STEPS, 2)), dma((STEPS, 2)),
            dma((STEPS, 2)), dma((STEPS, 2)),
            dma((STEPS, 4)), dma((STEPS, 4)),
            dma((STEPS, others)), dma((STEPS, others)),
            dma((STEPS, others)), dma((STEPS, others)),
        ],
        compiler_params=pltpu.CompilerParams(
            collective_id=0, has_side_effects=True, vmem_limit_bytes=40 << 20
        ),
        name="bgk",
    )(disp, frac, heat, particle_distributions.reshape(nv * ROWS, LANES), freq, solid)
    return out.reshape(nv, ROWS, LANES)


def solution(mesh):
    sizes = (mesh.shape["vel"], mesh.shape["sx"], mesh.shape["sy"])
    return jax.shard_map(
        functools.partial(per_device, sizes),
        mesh=mesh,
        in_specs=(
            P("vel", "sx", "sy"),
            P(None, "vel"),
            P(None, "vel"),
            P("sx", "sy"),
            P("sx", "sy"),
            P(),
        ),
        out_specs=P("vel", "sx", "sy"),
        check_vma=False,
    )
```

```python
import functools
import math

import jax
import jax.numpy as jnp
from jax import lax
from jax.experimental import pallas as pl
from jax.experimental.pallas import tpu as pltpu
from jax.sharding import PartitionSpec as P

MAXS = 4
STEPS = 2
ROWS = 8
LANES = 128
GROUP = 16
PART = 4
CHUNK = GROUP * PART
SPAN = 24
LOG2E = math.log2(math.e)
F32 = jnp.float32
BF16 = jnp.bfloat16


def kernel(
    sizes,
    heat,
    disp_in,
    frac_in,
    x_in,
    freq_in,
    solid_in,
    o_ref,
    disp,
    frac,
    x_ref,
    freq_ref,
    solid_ref,
    in_sem,
    ext,
    pext,
    pack_f,
    moved_ref,
    prof_ref,
    wall_ref,
    xsend,
    psend,
    csend,
    xrecv,
    precv,
    crecv,
    msend,
    mrecv,
    zsend,
    zrecv,
    xs_sem,
    xr_sem,
    ps_sem,
    pr_sem,
    cs_sem,
    cr_sem,
    ms_sem,
    mr_sem,
    zs_sem,
    zr_sem,
):
    nvel, nsx, nsy = sizes
    nv = disp.shape[1]
    chunks = nv // CHUNK
    loads = [
        pltpu.make_async_copy(src, dst, in_sem.at[i])
        for i, (src, dst) in enumerate(
            [(x_in, x_ref), (disp_in, disp), (frac_in, frac), (freq_in, freq_ref), (solid_in, solid_ref)]
        )
    ]
    for load in loads:
        load.start()
    vel = lax.axis_index("vel")
    sx = lax.axis_index("sx")
    sy = lax.axis_index("sy")
    up, down = lax.rem(sx + 1, nsx), lax.rem(sx + nsx - 1, nsx)
    right, left = lax.rem(sy + 1, nsy), lax.rem(sy + nsy - 1, nsy)
    peers = [lax.rem(vel + p, nvel) for p in range(1, nvel)]
    sources = [lax.rem(vel + nvel - p, nvel) for p in range(1, nvel)]

    def at(v, i, j):
        return (v, i, j)

    spatial = [
        at(vel, up, sy), at(vel, down, sy), at(vel, sx, right), at(vel, sx, left),
        at(vel, up, right), at(vel, up, left), at(vel, down, right), at(vel, down, left),
    ]
    barrier = pltpu.get_barrier_semaphore()
    for target in spatial + [at(p, sx, sy) for p in peers]:
        pl.semaphore_signal(barrier, inc=1, device_id=target, device_id_type=pl.DeviceIdType.MESH)

    lane = lax.broadcasted_iota(jnp.int32, (ROWS, LANES), 1)
    centered = jnp.where(lane < LANES // 2, lane, lane - LANES)
    slot = lane // 8
    from_left = lax.rem(lane, 8) < 4

    def remote(src, dst, send_sem, recv_sem, target):
        return pltpu.make_async_remote_copy(
            src_ref=src, dst_ref=dst, send_sem=send_sem, recv_sem=recv_sem,
            device_id=target, device_id_type=pl.DeviceIdType.MESH,
        )

    def halo_copies(step, c):
        rows = pl.ds(pl.multiple_of(c * (CHUNK * MAXS), 16), CHUNK * MAXS)
        prows = pl.ds(pl.multiple_of(c * (PART * ROWS), 16), PART * ROWS)
        crows = pl.ds(pl.multiple_of(c * (PART * MAXS), 16), PART * MAXS)
        copies = []
        for d in range(2):
            copies.append(remote(
                psend.at[step, prows], precv.at[step, d, prows],
                ps_sem.at[step, c, d], pr_sem.at[step, c, d], spatial[2 + d],
            ))
        for d in range(4):
            copies.append(remote(
                csend.at[step, d // 2, crows], crecv.at[step, d, crows],
                cs_sem.at[step, c, d], cr_sem.at[step, c, d], spatial[4 + d],
            ))
        for d in range(2):
            copies.append(remote(
                xsend.at[step, d, rows], xrecv.at[step, d, rows],
                xs_sem.at[step, c, d], xr_sem.at[step, c, d], spatial[d],
            ))
        return copies

    def stow(step, g, planes):
        packed = None
        for k, plane in enumerate(planes):
            ext[pl.ds(pl.multiple_of((g * GROUP + k) * SPAN, 8) + 8, ROWS), :] = plane
            turned = pltpu.roll(plane, (8 * k + 4) % LANES, 1)
            packed = turned if packed is None else jnp.where(slot == k, turned, packed)
        pack_f[pl.ds(pl.multiple_of(g * ROWS, 8), ROWS), :] = packed
        for q in range(GROUP // 4):
            four = planes[4 * q: 4 * q + 4]
            base = pl.multiple_of(g * (GROUP * 4) + q * 16, 16)
            xsend[step, 0, pl.ds(base, 16), :] = jnp.concatenate([f[4:8] for f in four], 0).astype(BF16)
            xsend[step, 1, pl.ds(base, 16), :] = jnp.concatenate([f[0:4] for f in four], 0).astype(BF16)

    def send_chunk(step, c):
        tops, bottoms, fulls = [], [], []
        for i in range(PART):
            plane = pack_f[pl.ds(pl.multiple_of((c * PART + i) * ROWS, 8), ROWS), :]
            tops.append(plane[4:8])
            bottoms.append(plane[0:4])
            fulls.append(plane)
        base = pl.multiple_of(c * (PART * MAXS), 16)
        csend[step, 0, pl.ds(base, 16), :] = jnp.concatenate(tops, 0).astype(BF16)
        csend[step, 1, pl.ds(base, 16), :] = jnp.concatenate(bottoms, 0).astype(BF16)
        base = pl.multiple_of(c * (PART * ROWS), 16)
        psend[step, pl.ds(base, PART * ROWS), :] = jnp.concatenate(fulls, 0).astype(BF16)
        for copy in halo_copies(step, c):
            copy.start()

    def receive_chunk(step, c):
        for copy in halo_copies(step, c):
            copy.wait_recv()

        def rows(i, carry):
            q = c * (CHUNK // 4) + i
            base = pl.multiple_of(q * 16, 16)
            low = xrecv[step, 0, pl.ds(base, 16), :].astype(F32)
            high = xrecv[step, 1, pl.ds(base, 16), :].astype(F32)
            for i in range(4):
                spot = pl.multiple_of((q * 4 + i) * SPAN, 8)
                ext[pl.ds(spot + 4, 4), :] = low[4 * i: 4 * i + 4]
                ext[pl.ds(spot + 16, 4), :] = high[4 * i: 4 * i + 4]
            return carry

        lax.fori_loop(0, CHUNK // 4, rows, 0, unroll=4)
        base = pl.multiple_of(c * (PART * ROWS), 16)
        a = precv[step, 0, pl.ds(base, PART * ROWS), :].astype(F32)
        b = precv[step, 1, pl.ds(base, PART * ROWS), :].astype(F32)
        base = pl.multiple_of(c * (PART * MAXS), 16)
        corners = [crecv[step, d, pl.ds(base, 16), :].astype(F32) for d in range(4)]
        pick = from_left[0:4]
        for i in range(PART):
            spot = pl.multiple_of((c * PART + i) * SPAN, 8)
            cut = slice(ROWS * i, ROWS * i + ROWS)
            pext[pl.ds(spot + 8, ROWS), :] = jnp.where(from_left, a[cut], b[cut])
            cut = slice(4 * i, 4 * i + 4)
            pext[pl.ds(spot + 4, 4), :] = jnp.where(pick, corners[0][cut], corners[1][cut])
            pext[pl.ds(spot + 16, 4), :] = jnp.where(pick, corners[2][cut], corners[3][cut])

    def speeds(v):
        return disp[0, v].astype(F32) + frac[0, v], disp[1, v].astype(F32) + frac[1, v]

    def source(main, side, shift):
        low, high = jnp.minimum(-shift, 0), jnp.maximum(-shift, 0)
        return jnp.where((centered >= low) & (centered < high), side, main)

    def turn(plane, shift):
        return pltpu.roll(plane, jnp.where(shift < 0, shift + LANES, shift), 1)

    def transport(g, k):
        v = g * GROUP + k
        mx, my = disp[0, v], disp[1, v]
        a, b = frac[0, v], frac[1, v]
        start = v * SPAN + 8 - mx
        main = (1.0 - a) * ext[pl.ds(start, ROWS), :] + a * ext[pl.ds(start - 1, ROWS), :]
        pstart = g * SPAN + 8 - mx
        side = (1.0 - a) * pext[pl.ds(pstart, ROWS), :] + a * pext[pl.ds(pstart - 1, ROWS), :]
        side = pltpu.roll(side, (2 * LANES - 8 * k - 4) % LANES, 1)
        near = turn(source(main, side, my), my)
        far = turn(source(main, side, my + 1), my + 1)
        return (1.0 - b) * near + b * far

    def add_over_vel(step, count, sref, rref, ssem, rsem, values):
        for i, value in enumerate(values):
            sref[step, i * ROWS: (i + 1) * ROWS, :] = value
        copies = [
            remote(sref.at[step], rref.at[step, p], ssem.at[step, p], rsem.at[step, p], at(peers[p], sx, sy))
            for p in range(nvel - 1)
        ]
        for copy in copies:
            copy.start()
        for copy in copies:
            copy.wait()
        totals = []
        for i, value in enumerate(values):
            for p in range(nvel - 1):
                value = value + rref[step, p, i * ROWS: (i + 1) * ROWS, :]
            totals.append(value)
        return totals

    groups = nv // GROUP
    zero = jnp.zeros((ROWS, LANES), F32)
    for load in loads:
        load.wait()
    pl.semaphore_wait(barrier, len(spatial) + nvel - 1)
    relax = 1.0 - jnp.exp(-freq_ref[...])
    solid = solid_ref[...] > 0
    wall_scale = -LOG2E / (2.0 * (zero + heat[0]))

    def load_group(g, carry):
        planes = []
        for k in range(0, GROUP, 2):
            pair = x_ref[pl.ds(pl.multiple_of(g * (GROUP * ROWS) + k * ROWS, 16), 16), :].astype(F32)
            planes += [pair[0:8], pair[8:16]]
        stow(0, g, planes)
        return carry

    def load_chunk(c, carry):
        lax.fori_loop(c * PART, (c + 1) * PART, load_group, 0)
        send_chunk(0, c)
        return carry

    lax.fori_loop(0, chunks, load_chunk, 0)

    wall_sum = None
    for step in range(STEPS):
        if step == 0:
            def wall_group(g, total):
                for k in range(GROUP):
                    v = g * GROUP + k
                    cx, cy = speeds(v)
                    w = jnp.exp2((cx * cx + cy * cy) * wall_scale)
                    wall_ref[pl.ds(pl.multiple_of(v * ROWS, 8), ROWS), :] = w
                    total = total + w
                return total

            wall_sum = lax.fori_loop(0, groups, wall_group, zero)

        def moment_group(g, carry):
            density, flux_x, flux_y, energy = carry
            for k in range(GROUP):
                v = g * GROUP + k
                cx, cy = speeds(v)
                moved = transport(g, k)
                moved_ref[pl.ds(pl.multiple_of(v * ROWS, 8), ROWS), :] = moved
                density = density + moved
                flux_x = flux_x + moved * cx
                flux_y = flux_y + moved * cy
                energy = energy + moved * (cx * cx + cy * cy)
            return density, flux_x, flux_y, energy

        def moment_chunk(c, carry):
            receive_chunk(step, c)
            return lax.fori_loop(c * PART, (c + 1) * PART, moment_group, carry)

        moments = list(lax.fori_loop(0, chunks, moment_chunk, (zero, zero, zero, zero)))
        extra = [wall_sum] if step == 0 else [zero]
        totals = add_over_vel(step, 5, msend, mrecv, ms_sem, mr_sem, moments + extra)
        density, flux_x, flux_y, energy = totals[:4]
        if step == 0:
            wall_sum = totals[4]
        drift_x = flux_x / density
        drift_y = flux_y / density
        thermal = 0.5 * (energy / density - drift_x * drift_x - drift_y * drift_y)
        scale = -LOG2E / (2.0 * thermal)

        def profile_group(g, total):
            for k in range(GROUP):
                v = g * GROUP + k
                cx, cy = speeds(v)
                off_x = cx - drift_x
                off_y = cy - drift_y
                value = jnp.exp2((off_x * off_x + off_y * off_y) * scale)
                prof_ref[pl.ds(pl.multiple_of(v * ROWS, 8), ROWS), :] = value
                total = total + value
            return total

        partition = lax.fori_loop(0, groups, profile_group, zero)
        (partition,) = add_over_vel(step, 1, zsend, zrecv, zs_sem, zr_sem, [partition])
        keep = 1.0 - relax
        gain = relax * density / partition
        wall_gain = density / wall_sum

        def relax_group(g, carry):
            planes = []
            for k in range(GROUP):
                rows = pl.ds(pl.multiple_of((g * GROUP + k) * ROWS, 8), ROWS)
                gas = keep * moved_ref[rows, :] + gain * prof_ref[rows, :]
                planes.append(jnp.where(solid, wall_gain * wall_ref[rows, :], gas))
            for k in range(0, GROUP, 2):
                pair = jnp.concatenate(planes[k: k + 2], 0).astype(BF16)
                if step == STEPS - 1:
                    o_ref[pl.ds(pl.multiple_of((g * GROUP + k) * ROWS, 16), 16), :] = pair
                else:
                    pair = pair.astype(F32)
                    planes[k: k + 2] = [pair[0:8], pair[8:16]]
            if step < STEPS - 1:
                stow(step + 1, g, planes)
            return carry

        def relax_chunk(c, carry):
            lax.fori_loop(c * PART, (c + 1) * PART, relax_group, 0)
            if step < STEPS - 1:
                send_chunk(step + 1, c)
            return carry

        lax.fori_loop(0, chunks, relax_chunk, 0)

    def drain(c, carry):
        for step in range(STEPS):
            for copy in halo_copies(step, c):
                copy.wait_send()
        return carry

    lax.fori_loop(0, chunks, drain, 0)


def per_device(sizes, particle_distributions, disp, frac, freq, solid, heat):
    nv, rows, lanes = particle_distributions.shape
    assert rows == ROWS and lanes == LANES and nv % CHUNK == 0
    nvel = sizes[0]
    others = max(nvel - 1, 1)
    groups = nv // GROUP
    chunks = nv // CHUNK
    dma = pltpu.SemaphoreType.DMA
    vmem = pl.BlockSpec(memory_space=pltpu.VMEM)
    hbm = pl.BlockSpec(memory_space=pltpu.MemorySpace.HBM)
    smem = pl.BlockSpec(memory_space=pltpu.SMEM)
    out = pl.pallas_call(
        functools.partial(kernel, sizes),
        out_shape=jax.ShapeDtypeStruct((nv * ROWS, LANES), BF16),
        in_specs=[smem, hbm, hbm, hbm, hbm, hbm],
        out_specs=vmem,
        scratch_shapes=[
            pltpu.SMEM((2, nv), jnp.int32),
            pltpu.SMEM((2, nv), F32),
            pltpu.VMEM((nv * ROWS, LANES), BF16),
            pltpu.VMEM((ROWS, LANES), F32),
            pltpu.VMEM((ROWS, LANES), jnp.int32),
            dma((5,)),
            pltpu.VMEM((nv * SPAN, LANES), F32),
            pltpu.VMEM((groups * SPAN, LANES), F32),
            pltpu.VMEM((groups * ROWS, LANES), F32),
            pltpu.VMEM((nv * ROWS, LANES), F32),
            pltpu.VMEM((nv * ROWS, LANES), F32),
            pltpu.VMEM((nv * ROWS, LANES), F32),
            pltpu.VMEM((STEPS, 2, nv * MAXS, LANES), BF16),
            pltpu.VMEM((STEPS, groups * ROWS, LANES), BF16),
            pltpu.VMEM((STEPS, 2, groups * MAXS, LANES), BF16),
            pltpu.VMEM((STEPS, 2, nv * MAXS, LANES), BF16),
            pltpu.VMEM((STEPS, 2, groups * ROWS, LANES), BF16),
            pltpu.VMEM((STEPS, 4, groups * MAXS, LANES), BF16),
            pltpu.VMEM((STEPS, 5 * ROWS, LANES), F32),
            pltpu.VMEM((STEPS, others, 5 * ROWS, LANES), F32),
            pltpu.VMEM((STEPS, ROWS, LANES), F32),
            pltpu.VMEM((STEPS, others, ROWS, LANES), F32),
            dma((STEPS, chunks, 2)), dma((STEPS, chunks, 2)),
            dma((STEPS, chunks, 2)), dma((STEPS, chunks, 2)),
            dma((STEPS, chunks, 4)), dma((STEPS, chunks, 4)),
            dma((STEPS, others)), dma((STEPS, others)),
            dma((STEPS, others)), dma((STEPS, others)),
        ],
        compiler_params=pltpu.CompilerParams(
            collective_id=0, has_side_effects=True, vmem_limit_bytes=63 << 20
        ),
        name="bgk",
    )(heat, disp, frac, particle_distributions.reshape(nv * ROWS, LANES), freq, solid)
    return out.reshape(nv, ROWS, LANES)


def solution(mesh):
    sizes = (mesh.shape["vel"], mesh.shape["sx"], mesh.shape["sy"])
    return jax.shard_map(
        functools.partial(per_device, sizes),
        mesh=mesh,
        in_specs=(
            P("vel", "sx", "sy"),
            P(None, "vel"),
            P(None, "vel"),
            P("sx", "sy"),
            P("sx", "sy"),
            P(),
        ),
        out_specs=P("vel", "sx", "sy"),
        check_vma=False,
    )
```

```python
import functools
import math

import jax
import jax.numpy as jnp
from jax import lax
from jax.experimental import pallas as pl
from jax.experimental.pallas import tpu as pltpu
from jax.sharding import PartitionSpec as P

MAXS = 4
STEPS = 2
ROWS = 8
LANES = 128
GROUP = 16
PART = 4
CHUNK = GROUP * PART
SPAN = 24
LOG2E = math.log2(math.e)
F32 = jnp.float32
BF16 = jnp.bfloat16


def kernel(
    sizes,
    general,
    heat,
    disp_in,
    frac_in,
    x_in,
    freq_in,
    solid_in,
    o_ref,
    flag_ref,
    disp,
    frac,
    x_ref,
    freq_ref,
    solid_ref,
    in_sem,
    ext,
    pext,
    pack_f,
    moved_ref,
    prof_ref,
    wall_ref,
    xsend,
    psend,
    csend,
    xrecv,
    precv,
    crecv,
    msend,
    mrecv,
    zsend,
    zrecv,
    xs_sem,
    xr_sem,
    ps_sem,
    pr_sem,
    cs_sem,
    cr_sem,
    ms_sem,
    mr_sem,
    zs_sem,
    zr_sem,
):
    nvel, nsx, nsy = sizes
    nv = disp.shape[1]
    chunks = nv // CHUNK
    loads = [
        pltpu.make_async_copy(src, dst, in_sem.at[i])
        for i, (src, dst) in enumerate(
            [(x_in, x_ref), (disp_in, disp), (frac_in, frac), (freq_in, freq_ref), (solid_in, solid_ref)]
        )
    ]
    for load in loads:
        load.start()
    vel = lax.axis_index("vel")
    sx = lax.axis_index("sx")
    sy = lax.axis_index("sy")
    up, down = lax.rem(sx + 1, nsx), lax.rem(sx + nsx - 1, nsx)
    right, left = lax.rem(sy + 1, nsy), lax.rem(sy + nsy - 1, nsy)
    peers = [lax.rem(vel + p, nvel) for p in range(1, nvel)]
    sources = [lax.rem(vel + nvel - p, nvel) for p in range(1, nvel)]

    def at(v, i, j):
        return (v, i, j)

    spatial = [
        at(vel, up, sy), at(vel, down, sy), at(vel, sx, right), at(vel, sx, left),
        at(vel, up, right), at(vel, up, left), at(vel, down, right), at(vel, down, left),
    ]
    barrier = pltpu.get_barrier_semaphore()
    for target in spatial + [at(p, sx, sy) for p in peers]:
        pl.semaphore_signal(barrier, inc=1, device_id=target, device_id_type=pl.DeviceIdType.MESH)

    lane = lax.broadcasted_iota(jnp.int32, (ROWS, LANES), 1)
    centered = jnp.where(lane < LANES // 2, lane, lane - LANES)
    slot = lane // 8
    from_left = lax.rem(lane, 8) < 4

    def remote(src, dst, send_sem, recv_sem, target):
        return pltpu.make_async_remote_copy(
            src_ref=src, dst_ref=dst, send_sem=send_sem, recv_sem=recv_sem,
            device_id=target, device_id_type=pl.DeviceIdType.MESH,
        )

    def reach(c):
        part = (vel * chunks + c) * (2 * MAXS) // (nvel * chunks)
        upward = jnp.where(part >= MAXS, jnp.minimum(part - MAXS + 2, MAXS), jnp.where(part == MAXS - 1, 1, 0))
        return upward, jnp.maximum(MAXS - part, 0)

    def lane_copies(step, c):
        prows = pl.ds(pl.multiple_of(c * (PART * ROWS), 16), PART * ROWS)
        crows = pl.ds(pl.multiple_of(c * (PART * MAXS), 16), PART * MAXS)
        copies = []
        for d in range(2):
            copies.append(remote(
                psend.at[step, prows], precv.at[step, d, prows],
                ps_sem.at[step, c, d], pr_sem.at[step, c, d], spatial[2 + d],
            ))
        for d in range(4):
            copies.append(remote(
                csend.at[step, d // 2, crows], crecv.at[step, d, crows],
                cs_sem.at[step, c, d], cr_sem.at[step, c, d], spatial[4 + d],
            ))
        return copies

    def row_copy(step, c, d, j):
        rows = pl.ds(pl.multiple_of(c * CHUNK, 16), CHUNK)
        return remote(
            xsend.at[step, d, j, rows], xrecv.at[step, d, j, rows],
            xs_sem.at[step, c, d, j], xr_sem.at[step, c, d, j], spatial[d],
        )

    def each_row(c, body):
        limits = reach(c)
        for d in range(2):
            for j in range(MAXS):
                if general:
                    body(d, j)
                else:
                    pl.when(j < limits[d])(functools.partial(body, d, j))

    def stow(step, g, planes):
        packed = None
        for k, plane in enumerate(planes):
            ext[pl.ds(pl.multiple_of((g * GROUP + k) * SPAN, 8) + 8, ROWS), :] = plane
            turned = pltpu.roll(plane, (8 * k + 4) % LANES, 1)
            packed = turned if packed is None else jnp.where(slot == k, turned, packed)
        pack_f[pl.ds(pl.multiple_of(g * ROWS, 8), ROWS), :] = packed

    def send_chunk(step, c):
        tops, bottoms, fulls = [], [], []
        for i in range(PART):
            plane = pack_f[pl.ds(pl.multiple_of((c * PART + i) * ROWS, 8), ROWS), :]
            tops.append(plane[4:8])
            bottoms.append(plane[0:4])
            fulls.append(plane)
        base = pl.multiple_of(c * (PART * MAXS), 16)
        csend[step, 0, pl.ds(base, 16), :] = jnp.concatenate(tops, 0).astype(BF16)
        csend[step, 1, pl.ds(base, 16), :] = jnp.concatenate(bottoms, 0).astype(BF16)
        base = pl.multiple_of(c * (PART * ROWS), 16)
        psend[step, pl.ds(base, PART * ROWS), :] = jnp.concatenate(fulls, 0).astype(BF16)
        for copy in lane_copies(step, c):
            copy.start()

        def send_row(d, j):
            row = ROWS + (ROWS - 1 - j if d == 0 else j)
            for i in range(CHUNK // 16):
                first = pl.multiple_of(c * (CHUNK * SPAN), 8) + i * (16 * SPAN) + row
                halves = [ext[pl.ds(first + h * (8 * SPAN), 8, stride=SPAN), :] for h in range(2)]
                spot = pl.multiple_of(c * CHUNK + i * 16, 16)
                xsend[step, d, j, pl.ds(spot, 16), :] = jnp.concatenate(halves, 0).astype(BF16)
            row_copy(step, c, d, j).start()

        each_row(c, send_row)

    def receive_chunk(step, c):
        for copy in lane_copies(step, c):
            copy.wait_recv()

        def receive_row(d, j):
            row_copy(step, c, d, j).wait_recv()
            row = ROWS - 1 - j if d == 0 else 2 * ROWS + j
            for i in range(CHUNK // 16):
                spot = pl.multiple_of(c * CHUNK + i * 16, 16)
                pair = xrecv[step, d, j, pl.ds(spot, 16), :].astype(F32)
                first = pl.multiple_of(c * (CHUNK * SPAN), 8) + i * (16 * SPAN) + row
                for h in range(2):
                    ext[pl.ds(first + h * (8 * SPAN), 8, stride=SPAN), :] = pair[8 * h: 8 * h + 8]

        each_row(c, receive_row)
        base = pl.multiple_of(c * (PART * ROWS), 16)
        a = precv[step, 0, pl.ds(base, PART * ROWS), :].astype(F32)
        b = precv[step, 1, pl.ds(base, PART * ROWS), :].astype(F32)
        base = pl.multiple_of(c * (PART * MAXS), 16)
        corners = [crecv[step, d, pl.ds(base, 16), :].astype(F32) for d in range(4)]
        pick = from_left[0:4]
        for i in range(PART):
            spot = pl.multiple_of((c * PART + i) * SPAN, 8)
            cut = slice(ROWS * i, ROWS * i + ROWS)
            pext[pl.ds(spot + 8, ROWS), :] = jnp.where(from_left, a[cut], b[cut])
            cut = slice(4 * i, 4 * i + 4)
            pext[pl.ds(spot + 4, 4), :] = jnp.where(pick, corners[0][cut], corners[1][cut])
            pext[pl.ds(spot + 16, 4), :] = jnp.where(pick, corners[2][cut], corners[3][cut])

    def speeds(v):
        return disp[0, v].astype(F32) + frac[0, v], disp[1, v].astype(F32) + frac[1, v]

    def source(main, side, shift):
        low, high = jnp.minimum(-shift, 0), jnp.maximum(-shift, 0)
        return jnp.where((centered >= low) & (centered < high), side, main)

    def turn(plane, shift):
        return pltpu.roll(plane, jnp.where(shift < 0, shift + LANES, shift), 1)

    def transport(g, k):
        v = g * GROUP + k
        mx, my = disp[0, v], disp[1, v]
        a, b = frac[0, v], frac[1, v]
        start = v * SPAN + 8 - mx
        main = (1.0 - a) * ext[pl.ds(start, ROWS), :] + a * ext[pl.ds(start - 1, ROWS), :]
        pstart = g * SPAN + 8 - mx
        side = (1.0 - a) * pext[pl.ds(pstart, ROWS), :] + a * pext[pl.ds(pstart - 1, ROWS), :]
        side = pltpu.roll(side, (2 * LANES - 8 * k - 4) % LANES, 1)
        near = turn(source(main, side, my), my)
        far = turn(source(main, side, my + 1), my + 1)
        return (1.0 - b) * near + b * far

    def add_over_vel(step, count, sref, rref, ssem, rsem, values):
        for i, value in enumerate(values):
            sref[step, i * ROWS: (i + 1) * ROWS, :] = value
        copies = [
            remote(sref.at[step], rref.at[step, p], ssem.at[step, p], rsem.at[step, p], at(peers[p], sx, sy))
            for p in range(nvel - 1)
        ]
        for copy in copies:
            copy.start()
        for copy in copies:
            copy.wait()
        totals = []
        for i, value in enumerate(values):
            for p in range(nvel - 1):
                value = value + rref[step, p, i * ROWS: (i + 1) * ROWS, :]
            totals.append(value)
        return totals

    groups = nv // GROUP
    zero = jnp.zeros((ROWS, LANES), F32)
    for load in loads:
        load.wait()
    pl.semaphore_wait(barrier, len(spatial) + nvel - 1)
    relax = 1.0 - jnp.exp(-freq_ref[...])
    solid = solid_ref[...] > 0
    wall_scale = -LOG2E / (2.0 * (zero + heat[0]))

    def load_group(g, carry):
        planes = []
        for k in range(0, GROUP, 2):
            pair = x_ref[pl.ds(pl.multiple_of(g * (GROUP * ROWS) + k * ROWS, 16), 16), :].astype(F32)
            planes += [pair[0:8], pair[8:16]]
        stow(0, g, planes)
        return carry

    def load_chunk(c, carry):
        lax.fori_loop(c * PART, (c + 1) * PART, load_group, 0)
        send_chunk(0, c)
        return carry

    lax.fori_loop(0, chunks, load_chunk, 0)

    wall_sum = None
    for step in range(STEPS):
        if step == 0:
            def wall_group(g, carry):
                total, beyond = carry
                upward, downward = reach(g // PART)
                for k in range(GROUP):
                    v = g * GROUP + k
                    beyond = jnp.maximum(beyond, jnp.where(disp[0, v] < 0, -disp[0, v] - downward, disp[0, v] + 1 - upward))
                    cx, cy = speeds(v)
                    w = jnp.exp2((cx * cx + cy * cy) * wall_scale)
                    wall_ref[pl.ds(pl.multiple_of(v * ROWS, 8), ROWS), :] = w
                    total = total + w
                return total, beyond

            wall_sum, beyond = lax.fori_loop(0, groups, wall_group, (zero, jnp.int32(0)))

        def moment_group(g, carry):
            density, flux_x, flux_y, energy = carry
            for k in range(GROUP):
                v = g * GROUP + k
                cx, cy = speeds(v)
                moved = transport(g, k)
                moved_ref[pl.ds(pl.multiple_of(v * ROWS, 8), ROWS), :] = moved
                density = density + moved
                flux_x = flux_x + moved * cx
                flux_y = flux_y + moved * cy
                energy = energy + moved * (cx * cx + cy * cy)
            return density, flux_x, flux_y, energy

        def moment_chunk(c, carry):
            receive_chunk(step, c)
            return lax.fori_loop(c * PART, (c + 1) * PART, moment_group, carry)

        moments = list(lax.fori_loop(0, chunks, moment_chunk, (zero, zero, zero, zero)))
        extra = [wall_sum, zero + beyond.astype(F32)] if step == 0 else [zero, zero]
        totals = add_over_vel(step, 6, msend, mrecv, ms_sem, mr_sem, moments + extra)
        density, flux_x, flux_y, energy = totals[:4]
        if step == 0:
            wall_sum = totals[4]
            flag_ref[...] = totals[5]
        drift_x = flux_x / density
        drift_y = flux_y / density
        thermal = 0.5 * (energy / density - drift_x * drift_x - drift_y * drift_y)
        scale = -LOG2E / (2.0 * thermal)

        def profile_group(g, total):
            for k in range(GROUP):
                v = g * GROUP + k
                cx, cy = speeds(v)
                off_x = cx - drift_x
                off_y = cy - drift_y
                value = jnp.exp2((off_x * off_x + off_y * off_y) * scale)
                prof_ref[pl.ds(pl.multiple_of(v * ROWS, 8), ROWS), :] = value
                total = total + value
            return total

        partition = lax.fori_loop(0, groups, profile_group, zero)
        (partition,) = add_over_vel(step, 1, zsend, zrecv, zs_sem, zr_sem, [partition])
        keep = 1.0 - relax
        gain = relax * density / partition
        wall_gain = density / wall_sum

        def relax_group(g, carry):
            planes = []
            for k in range(GROUP):
                rows = pl.ds(pl.multiple_of((g * GROUP + k) * ROWS, 8), ROWS)
                gas = keep * moved_ref[rows, :] + gain * prof_ref[rows, :]
                planes.append(jnp.where(solid, wall_gain * wall_ref[rows, :], gas))
            for k in range(0, GROUP, 2):
                pair = jnp.concatenate(planes[k: k + 2], 0).astype(BF16)
                if step == STEPS - 1:
                    o_ref[pl.ds(pl.multiple_of((g * GROUP + k) * ROWS, 16), 16), :] = pair
                else:
                    pair = pair.astype(F32)
                    planes[k: k + 2] = [pair[0:8], pair[8:16]]
            if step < STEPS - 1:
                stow(step + 1, g, planes)
            return carry

        def relax_chunk(c, carry):
            lax.fori_loop(c * PART, (c + 1) * PART, relax_group, 0)
            if step < STEPS - 1:
                send_chunk(step + 1, c)
            return carry

        lax.fori_loop(0, chunks, relax_chunk, 0)

    def drain(c, carry):
        for step in range(STEPS):
            for copy in lane_copies(step, c):
                copy.wait_send()
            each_row(c, lambda d, j: row_copy(step, c, d, j).wait_send())
        return carry

    lax.fori_loop(0, chunks, drain, 0)


def per_device(sizes, particle_distributions, disp, frac, freq, solid, heat):
    nv, rows, lanes = particle_distributions.shape
    assert rows == ROWS and lanes == LANES and nv % CHUNK == 0
    nvel = sizes[0]
    others = max(nvel - 1, 1)
    groups = nv // GROUP
    chunks = nv // CHUNK
    dma = pltpu.SemaphoreType.DMA
    vmem = pl.BlockSpec(memory_space=pltpu.VMEM)
    hbm = pl.BlockSpec(memory_space=pltpu.MemorySpace.HBM)
    smem = pl.BlockSpec(memory_space=pltpu.SMEM)
    def call(general):
        return pl.pallas_call(
        functools.partial(kernel, sizes, general),
        out_shape=(
            jax.ShapeDtypeStruct((nv * ROWS, LANES), BF16),
            jax.ShapeDtypeStruct((ROWS, LANES), F32),
        ),
        in_specs=[smem, hbm, hbm, hbm, hbm, hbm],
        out_specs=(vmem, vmem),
        scratch_shapes=[
            pltpu.SMEM((2, nv), jnp.int32),
            pltpu.SMEM((2, nv), F32),
            pltpu.VMEM((nv * ROWS, LANES), BF16),
            pltpu.VMEM((ROWS, LANES), F32),
            pltpu.VMEM((ROWS, LANES), jnp.int32),
            dma((5,)),
            pltpu.VMEM((nv * SPAN, LANES), F32),
            pltpu.VMEM((groups * SPAN, LANES), F32),
            pltpu.VMEM((groups * ROWS, LANES), F32),
            pltpu.VMEM((nv * ROWS, LANES), F32),
            pltpu.VMEM((nv * ROWS, LANES), F32),
            pltpu.VMEM((nv * ROWS, LANES), F32),
            pltpu.VMEM((STEPS, 2, MAXS, nv, LANES), BF16),
            pltpu.VMEM((STEPS, groups * ROWS, LANES), BF16),
            pltpu.VMEM((STEPS, 2, groups * MAXS, LANES), BF16),
            pltpu.VMEM((STEPS, 2, MAXS, nv, LANES), BF16),
            pltpu.VMEM((STEPS, 2, groups * ROWS, LANES), BF16),
            pltpu.VMEM((STEPS, 4, groups * MAXS, LANES), BF16),
            pltpu.VMEM((STEPS, 6 * ROWS, LANES), F32),
            pltpu.VMEM((STEPS, others, 6 * ROWS, LANES), F32),
            pltpu.VMEM((STEPS, ROWS, LANES), F32),
            pltpu.VMEM((STEPS, others, ROWS, LANES), F32),
            dma((STEPS, chunks, 2, MAXS)), dma((STEPS, chunks, 2, MAXS)),
            dma((STEPS, chunks, 2)), dma((STEPS, chunks, 2)),
            dma((STEPS, chunks, 4)), dma((STEPS, chunks, 4)),
            dma((STEPS, others)), dma((STEPS, others)),
            dma((STEPS, others)), dma((STEPS, others)),
        ],
        compiler_params=pltpu.CompilerParams(
            collective_id=int(general), has_side_effects=True, vmem_limit_bytes=63 << 20
        ),
        name="bgk_general" if general else "bgk",
    )(*operands)

    operands = (heat, disp, frac, particle_distributions.reshape(nv * ROWS, LANES), freq, solid)
    out, flag = call(False)
    out = lax.cond(flag[0, 0] > 0.0, lambda: call(True)[0], lambda: out)
    return out.reshape(nv, ROWS, LANES)


def solution(mesh):
    sizes = (mesh.shape["vel"], mesh.shape["sx"], mesh.shape["sy"])
    return jax.shard_map(
        functools.partial(per_device, sizes),
        mesh=mesh,
        in_specs=(
            P("vel", "sx", "sy"),
            P(None, "vel"),
            P(None, "vel"),
            P("sx", "sy"),
            P("sx", "sy"),
            P(),
        ),
        out_specs=P("vel", "sx", "sy"),
        check_vma=False,
    )
```

```python
import functools
import math

import jax
import jax.numpy as jnp
from jax import lax
from jax.experimental import pallas as pl
from jax.experimental.pallas import tpu as pltpu
from jax.sharding import PartitionSpec as P

MAXS = 4
STEPS = 2
ROWS = 8
LANES = 128
GROUP = 16
PART = 4
CHUNK = GROUP * PART
SPAN = 24
LOG2E = math.log2(math.e)
F32 = jnp.float32
BF16 = jnp.bfloat16


def kernel(
    sizes,
    general,
    heat,
    disp_in,
    frac_in,
    x_in,
    freq_in,
    solid_in,
    o_hbm,
    flag_ref,
    o_ref,
    out_sem,
    disp,
    frac,
    x_ref,
    freq_ref,
    solid_ref,
    in_sem,
    ext,
    pext,
    pack_f,
    moved_ref,
    prof_ref,
    wall_ref,
    xsend,
    psend,
    csend,
    xrecv,
    precv,
    crecv,
    msend,
    mrecv,
    zsend,
    zrecv,
    xs_sem,
    xr_sem,
    ps_sem,
    pr_sem,
    cs_sem,
    cr_sem,
    ms_sem,
    mr_sem,
    zs_sem,
    zr_sem,
):
    nvel, nsx, nsy = sizes
    nv = disp.shape[1]
    chunks = nv // CHUNK
    loads = [
        pltpu.make_async_copy(src, dst, in_sem.at[i])
        for i, (src, dst) in enumerate(
            [(x_in, x_ref), (disp_in, disp), (frac_in, frac), (freq_in, freq_ref), (solid_in, solid_ref)]
        )
    ]
    for load in loads:
        load.start()
    vel = lax.axis_index("vel")
    sx = lax.axis_index("sx")
    sy = lax.axis_index("sy")
    up, down = lax.rem(sx + 1, nsx), lax.rem(sx + nsx - 1, nsx)
    right, left = lax.rem(sy + 1, nsy), lax.rem(sy + nsy - 1, nsy)
    peers = [lax.rem(vel + p, nvel) for p in range(1, nvel)]
    sources = [lax.rem(vel + nvel - p, nvel) for p in range(1, nvel)]

    def at(v, i, j):
        return (v, i, j)

    spatial = [
        at(vel, up, sy), at(vel, down, sy), at(vel, sx, right), at(vel, sx, left),
        at(vel, up, right), at(vel, up, left), at(vel, down, right), at(vel, down, left),
    ]
    barrier = pltpu.get_barrier_semaphore()
    for target in spatial + [at(p, sx, sy) for p in peers]:
        pl.semaphore_signal(barrier, inc=1, device_id=target, device_id_type=pl.DeviceIdType.MESH)

    lane = lax.broadcasted_iota(jnp.int32, (ROWS, LANES), 1)
    centered = jnp.where(lane < LANES // 2, lane, lane - LANES)
    slot = lane // 8
    from_left = lax.rem(lane, 8) < 4

    def remote(src, dst, send_sem, recv_sem, target):
        return pltpu.make_async_remote_copy(
            src_ref=src, dst_ref=dst, send_sem=send_sem, recv_sem=recv_sem,
            device_id=target, device_id_type=pl.DeviceIdType.MESH,
        )

    def reach(c):
        part = (vel * chunks + c) * (2 * MAXS) // (nvel * chunks)
        upward = jnp.where(part >= MAXS, jnp.minimum(part - MAXS + 2, MAXS), jnp.where(part == MAXS - 1, 1, 0))
        return upward, jnp.maximum(MAXS - part, 0)

    def out_copy(c):
        rows = pl.ds(pl.multiple_of(c * (CHUNK * ROWS), 16), CHUNK * ROWS)
        return pltpu.make_async_copy(o_ref.at[rows], o_hbm.at[rows], out_sem.at[c])

    def lane_copies(step, c):
        prows = pl.ds(pl.multiple_of(c * (PART * ROWS), 16), PART * ROWS)
        crows = pl.ds(pl.multiple_of(c * (PART * MAXS), 16), PART * MAXS)
        copies = []
        for d in range(2):
            copies.append(remote(
                psend.at[step, prows], precv.at[step, d, prows],
                ps_sem.at[step, c, d], pr_sem.at[step, c, d], spatial[2 + d],
            ))
        for d in range(4):
            copies.append(remote(
                csend.at[step, d // 2, crows], crecv.at[step, d, crows],
                cs_sem.at[step, c, d], cr_sem.at[step, c, d], spatial[4 + d],
            ))
        return copies

    def row_copy(step, c, d, j):
        rows = pl.ds(pl.multiple_of(c * CHUNK, 16), CHUNK)
        return remote(
            xsend.at[step, d, j, rows], xrecv.at[step, d, j, rows],
            xs_sem.at[step, c, d, j], xr_sem.at[step, c, d, j], spatial[d],
        )

    def each_row(c, body):
        limits = reach(c)
        for d in range(2):
            for j in range(MAXS):
                if general:
                    body(d, j)
                else:
                    pl.when(j < limits[d])(functools.partial(body, d, j))

    def stow(step, g, planes):
        packed = None
        for k, plane in enumerate(planes):
            ext[pl.ds(pl.multiple_of((g * GROUP + k) * SPAN, 8) + 8, ROWS), :] = plane
            turned = pltpu.roll(plane, (8 * k + 4) % LANES, 1)
            packed = turned if packed is None else jnp.where(slot == k, turned, packed)
        pack_f[pl.ds(pl.multiple_of(g * ROWS, 8), ROWS), :] = packed

    def send_chunk(step, c):
        tops, bottoms, fulls = [], [], []
        for i in range(PART):
            plane = pack_f[pl.ds(pl.multiple_of((c * PART + i) * ROWS, 8), ROWS), :]
            tops.append(plane[4:8])
            bottoms.append(plane[0:4])
            fulls.append(plane)
        base = pl.multiple_of(c * (PART * MAXS), 16)
        csend[step, 0, pl.ds(base, 16), :] = jnp.concatenate(tops, 0).astype(BF16)
        csend[step, 1, pl.ds(base, 16), :] = jnp.concatenate(bottoms, 0).astype(BF16)
        base = pl.multiple_of(c * (PART * ROWS), 16)
        psend[step, pl.ds(base, PART * ROWS), :] = jnp.concatenate(fulls, 0).astype(BF16)
        for copy in lane_copies(step, c):
            copy.start()

        def send_row(d, j):
            row = ROWS + (ROWS - 1 - j if d == 0 else j)
            for i in range(CHUNK // 16):
                first = pl.multiple_of(c * (CHUNK * SPAN), 8) + i * (16 * SPAN) + row
                halves = [ext[pl.ds(first + h * (8 * SPAN), 8, stride=SPAN), :] for h in range(2)]
                spot = pl.multiple_of(c * CHUNK + i * 16, 16)
                xsend[step, d, j, pl.ds(spot, 16), :] = jnp.concatenate(halves, 0).astype(BF16)
            row_copy(step, c, d, j).start()

        each_row(c, send_row)

    def receive_chunk(step, c):
        for copy in lane_copies(step, c):
            copy.wait_recv()

        def receive_row(d, j):
            row_copy(step, c, d, j).wait_recv()
            row = ROWS - 1 - j if d == 0 else 2 * ROWS + j
            for i in range(CHUNK // 16):
                spot = pl.multiple_of(c * CHUNK + i * 16, 16)
                pair = xrecv[step, d, j, pl.ds(spot, 16), :].astype(F32)
                first = pl.multiple_of(c * (CHUNK * SPAN), 8) + i * (16 * SPAN) + row
                for h in range(2):
                    ext[pl.ds(first + h * (8 * SPAN), 8, stride=SPAN), :] = pair[8 * h: 8 * h + 8]

        each_row(c, receive_row)
        base = pl.multiple_of(c * (PART * ROWS), 16)
        a = precv[step, 0, pl.ds(base, PART * ROWS), :].astype(F32)
        b = precv[step, 1, pl.ds(base, PART * ROWS), :].astype(F32)
        base = pl.multiple_of(c * (PART * MAXS), 16)
        corners = [crecv[step, d, pl.ds(base, 16), :].astype(F32) for d in range(4)]
        pick = from_left[0:4]
        for i in range(PART):
            spot = pl.multiple_of((c * PART + i) * SPAN, 8)
            cut = slice(ROWS * i, ROWS * i + ROWS)
            pext[pl.ds(spot + 8, ROWS), :] = jnp.where(from_left, a[cut], b[cut])
            cut = slice(4 * i, 4 * i + 4)
            pext[pl.ds(spot + 4, 4), :] = jnp.where(pick, corners[0][cut], corners[1][cut])
            pext[pl.ds(spot + 16, 4), :] = jnp.where(pick, corners[2][cut], corners[3][cut])

    def speeds(v):
        return disp[0, v].astype(F32) + frac[0, v], disp[1, v].astype(F32) + frac[1, v]

    def source(main, side, shift):
        low, high = jnp.minimum(-shift, 0), jnp.maximum(-shift, 0)
        return jnp.where((centered >= low) & (centered < high), side, main)

    def turn(plane, shift):
        return pltpu.roll(plane, jnp.where(shift < 0, shift + LANES, shift), 1)

    def transport(g, k):
        v = g * GROUP + k
        mx, my = disp[0, v], disp[1, v]
        a, b = frac[0, v], frac[1, v]
        start = v * SPAN + 8 - mx
        main = (1.0 - a) * ext[pl.ds(start, ROWS), :] + a * ext[pl.ds(start - 1, ROWS), :]
        pstart = g * SPAN + 8 - mx
        side = (1.0 - a) * pext[pl.ds(pstart, ROWS), :] + a * pext[pl.ds(pstart - 1, ROWS), :]
        side = pltpu.roll(side, (2 * LANES - 8 * k - 4) % LANES, 1)
        near = turn(source(main, side, my), my)
        far = turn(source(main, side, my + 1), my + 1)
        return (1.0 - b) * near + b * far

    def add_over_vel(step, count, sref, rref, ssem, rsem, values):
        for i, value in enumerate(values):
            sref[step, i * ROWS: (i + 1) * ROWS, :] = value
        copies = [
            remote(sref.at[step], rref.at[step, p], ssem.at[step, p], rsem.at[step, p], at(peers[p], sx, sy))
            for p in range(nvel - 1)
        ]
        for copy in copies:
            copy.start()
        for copy in copies:
            copy.wait()
        totals = []
        for i, value in enumerate(values):
            for p in range(nvel - 1):
                value = value + rref[step, p, i * ROWS: (i + 1) * ROWS, :]
            totals.append(value)
        return totals

    groups = nv // GROUP
    zero = jnp.zeros((ROWS, LANES), F32)
    for load in loads:
        load.wait()
    pl.semaphore_wait(barrier, len(spatial) + nvel - 1)
    relax = 1.0 - jnp.exp(-freq_ref[...])
    solid = solid_ref[...] > 0
    wall_scale = -LOG2E / (2.0 * (zero + heat[0]))

    def load_group(g, carry):
        planes = []
        for k in range(0, GROUP, 2):
            pair = x_ref[pl.ds(pl.multiple_of(g * (GROUP * ROWS) + k * ROWS, 16), 16), :].astype(F32)
            planes += [pair[0:8], pair[8:16]]
        stow(0, g, planes)
        return carry

    def load_chunk(c, carry):
        lax.fori_loop(c * PART, (c + 1) * PART, load_group, 0)
        send_chunk(0, c)
        return carry

    lax.fori_loop(0, chunks, load_chunk, 0)

    wall_sum = None
    for step in range(STEPS):
        if step == 0:
            def wall_group(g, carry):
                total, beyond = carry
                upward, downward = reach(g // PART)
                for k in range(GROUP):
                    v = g * GROUP + k
                    beyond = jnp.maximum(beyond, jnp.where(disp[0, v] < 0, -disp[0, v] - downward, disp[0, v] + 1 - upward))
                    cx, cy = speeds(v)
                    w = jnp.exp2((cx * cx + cy * cy) * wall_scale)
                    wall_ref[pl.ds(pl.multiple_of(v * ROWS, 8), ROWS), :] = w
                    total = total + w
                return total, beyond

            wall_sum, beyond = lax.fori_loop(0, groups, wall_group, (zero, jnp.int32(0)))

        def moment_group(g, carry):
            density, flux_x, flux_y, energy = carry
            for k in range(GROUP):
                v = g * GROUP + k
                cx, cy = speeds(v)
                moved = transport(g, k)
                moved_ref[pl.ds(pl.multiple_of(v * ROWS, 8), ROWS), :] = moved
                density = density + moved
                flux_x = flux_x + moved * cx
                flux_y = flux_y + moved * cy
                energy = energy + moved * (cx * cx + cy * cy)
            return density, flux_x, flux_y, energy

        def moment_chunk(c, carry):
            receive_chunk(step, c)
            return lax.fori_loop(c * PART, (c + 1) * PART, moment_group, carry)

        moments = list(lax.fori_loop(0, chunks, moment_chunk, (zero, zero, zero, zero)))
        extra = [wall_sum, zero + beyond.astype(F32)] if step == 0 else [zero, zero]
        totals = add_over_vel(step, 6, msend, mrecv, ms_sem, mr_sem, moments + extra)
        density, flux_x, flux_y, energy = totals[:4]
        if step == 0:
            wall_sum = totals[4]
            flag_ref[...] = totals[5][0:1, 0:1]
        drift_x = flux_x / density
        drift_y = flux_y / density
        thermal = 0.5 * (energy / density - drift_x * drift_x - drift_y * drift_y)
        scale = -LOG2E / (2.0 * thermal)

        def profile_group(g, total):
            for k in range(GROUP):
                v = g * GROUP + k
                cx, cy = speeds(v)
                off_x = cx - drift_x
                off_y = cy - drift_y
                value = jnp.exp2((off_x * off_x + off_y * off_y) * scale)
                prof_ref[pl.ds(pl.multiple_of(v * ROWS, 8), ROWS), :] = value
                total = total + value
            return total

        partition = lax.fori_loop(0, groups, profile_group, zero)
        (partition,) = add_over_vel(step, 1, zsend, zrecv, zs_sem, zr_sem, [partition])
        keep = 1.0 - relax
        gain = relax * density / partition
        wall_gain = density / wall_sum

        def relax_group(g, carry):
            planes = []
            for k in range(GROUP):
                rows = pl.ds(pl.multiple_of((g * GROUP + k) * ROWS, 8), ROWS)
                gas = keep * moved_ref[rows, :] + gain * prof_ref[rows, :]
                planes.append(jnp.where(solid, wall_gain * wall_ref[rows, :], gas))
            for k in range(0, GROUP, 2):
                pair = jnp.concatenate(planes[k: k + 2], 0).astype(BF16)
                if step == STEPS - 1:
                    o_ref[pl.ds(pl.multiple_of((g * GROUP + k) * ROWS, 16), 16), :] = pair
                else:
                    pair = pair.astype(F32)
                    planes[k: k + 2] = [pair[0:8], pair[8:16]]
            if step < STEPS - 1:
                stow(step + 1, g, planes)
            return carry

        def relax_chunk(c, carry):
            lax.fori_loop(c * PART, (c + 1) * PART, relax_group, 0)
            if step < STEPS - 1:
                send_chunk(step + 1, c)
            else:
                out_copy(c).start()
            return carry

        lax.fori_loop(0, chunks, relax_chunk, 0)

    def drain(c, carry):
        out_copy(c).wait()
        for step in range(STEPS):
            for copy in lane_copies(step, c):
                copy.wait_send()
            each_row(c, lambda d, j: row_copy(step, c, d, j).wait_send())
        return carry

    lax.fori_loop(0, chunks, drain, 0)


def per_device(sizes, particle_distributions, disp, frac, freq, solid, heat):
    nv, rows, lanes = particle_distributions.shape
    assert rows == ROWS and lanes == LANES and nv % CHUNK == 0
    nvel = sizes[0]
    others = max(nvel - 1, 1)
    groups = nv // GROUP
    chunks = nv // CHUNK
    dma = pltpu.SemaphoreType.DMA
    vmem = pl.BlockSpec(memory_space=pltpu.VMEM)
    hbm = pl.BlockSpec(memory_space=pltpu.MemorySpace.HBM)
    smem = pl.BlockSpec(memory_space=pltpu.SMEM)
    def call(general):
        return pl.pallas_call(
        functools.partial(kernel, sizes, general),
        out_shape=(
            jax.ShapeDtypeStruct((nv * ROWS, LANES), BF16),
            jax.ShapeDtypeStruct((1, 1), F32),
        ),
        in_specs=[smem, hbm, hbm, hbm, hbm, hbm],
        out_specs=(hbm, vmem),
        scratch_shapes=[
            pltpu.VMEM((nv * ROWS, LANES), BF16),
            dma((chunks,)),
            pltpu.SMEM((2, nv), jnp.int32),
            pltpu.SMEM((2, nv), F32),
            pltpu.VMEM((nv * ROWS, LANES), BF16),
            pltpu.VMEM((ROWS, LANES), F32),
            pltpu.VMEM((ROWS, LANES), jnp.int32),
            dma((5,)),
            pltpu.VMEM((nv * SPAN, LANES), F32),
            pltpu.VMEM((groups * SPAN, LANES), F32),
            pltpu.VMEM((groups * ROWS, LANES), F32),
            pltpu.VMEM((nv * ROWS, LANES), F32),
            pltpu.VMEM((nv * ROWS, LANES), F32),
            pltpu.VMEM((nv * ROWS, LANES), F32),
            pltpu.VMEM((STEPS, 2, MAXS, nv, LANES), BF16),
            pltpu.VMEM((STEPS, groups * ROWS, LANES), BF16),
            pltpu.VMEM((STEPS, 2, groups * MAXS, LANES), BF16),
            pltpu.VMEM((STEPS, 2, MAXS, nv, LANES), BF16),
            pltpu.VMEM((STEPS, 2, groups * ROWS, LANES), BF16),
            pltpu.VMEM((STEPS, 4, groups * MAXS, LANES), BF16),
            pltpu.VMEM((STEPS, 6 * ROWS, LANES), F32),
            pltpu.VMEM((STEPS, others, 6 * ROWS, LANES), F32),
            pltpu.VMEM((STEPS, ROWS, LANES), F32),
            pltpu.VMEM((STEPS, others, ROWS, LANES), F32),
            dma((STEPS, chunks, 2, MAXS)), dma((STEPS, chunks, 2, MAXS)),
            dma((STEPS, chunks, 2)), dma((STEPS, chunks, 2)),
            dma((STEPS, chunks, 4)), dma((STEPS, chunks, 4)),
            dma((STEPS, others)), dma((STEPS, others)),
            dma((STEPS, others)), dma((STEPS, others)),
        ],
        compiler_params=pltpu.CompilerParams(
            collective_id=int(general), has_side_effects=True, vmem_limit_bytes=63 << 20
        ),
        name="bgk_general" if general else "bgk",
    )(*operands)

    operands = (heat, disp, frac, particle_distributions.reshape(nv * ROWS, LANES), freq, solid)
    out, flag = call(False)
    out = lax.cond(flag.reshape(()) > 0.0, lambda: call(True)[0], lambda: out)
    return out.reshape(nv, ROWS, LANES)


def solution(mesh):
    sizes = (mesh.shape["vel"], mesh.shape["sx"], mesh.shape["sy"])
    return jax.shard_map(
        functools.partial(per_device, sizes),
        mesh=mesh,
        in_specs=(
            P("vel", "sx", "sy"),
            P(None, "vel"),
            P(None, "vel"),
            P("sx", "sy"),
            P("sx", "sy"),
            P(),
        ),
        out_specs=P("vel", "sx", "sy"),
        check_vma=False,
    )
```
